32 devices in a mesh: groups: 2 (over x), seq: 16 (over z, y, core).
Axes of the slice: x: 2, y: 2, z: 4, core: 2. Of those that a mesh axis runs over, the one named last changes fastest.
Arguments:
- frames: bfloat16 [16384, 1024], P(('groups', 'seq')), parts along dimension 0, may hold values from -6 to 6
- context: bfloat16 [3072, 512], P(('groups', 'seq')), parts along dimension 0, may hold values from -6 to 6
- noise_level: int32 [128], P(('groups', 'seq')), parts along dimension 0, may hold values from 0 to 7
- alignment: int32 [128, 2], P(('groups', 'seq')), parts along dimension 0, may hold values from 0 to 31, as said below
- counts: int32 [128], P(('groups', 'seq')), parts along dimension 0, may hold values from 1 to 2
- band_width: int32 [16], replicated, may hold values from 0 to 2, as said below
- mod_table: float32 [8, 2048], replicated, may hold values from -3 to 3
- qkv_weight: bfloat16 [1024, 3072], replicated, may hold values from -0.1875 to 0.1875
- out_weight: bfloat16 [1024, 1024], replicated, may hold values from -0.1875 to 0.1875
- cross_query_weight: bfloat16 [1024, 512], replicated, may hold values from -0.1875 to 0.1875
- cross_kv_weight: bfloat16 [512, 1024], replicated, may hold values from -0.25 to 0.25
- cross_out_weight: bfloat16 [512, 1024], replicated, may hold values from -0.25 to 0.25
- banded_attender_factor: float32 [16], replicated, may hold values from 0.5 to 80
- cross_temp: float32 [8], replicated, may hold values from 0.5 to 80
Outputs:
- update: bfloat16 [16384, 1024], P(('groups', 'seq')), parts along dimension 0
The draws below stay inside these ranges and needn't reach their ends.
There are 2 independent parts, one for each index of `groups`. The reference program is written for one: setup_inputs(seed, part) draws one part's arguments, and reference() takes and returns one part's arrays. A program takes and returns all parts, laid end to end along the dimension named above; an argument that names none is the same for every part. Nothing has to cross between parts.
Inputs may be any that keep to these rules, and one draw needn't show every extreme that they name: `alignment`: the entries of each list are distinct consecutive token blocks, all within 1 token blocks of (b * 2) // 4 for frame block b. Among the rows of one device, the list of the first frame block starts as low as that allows and the list of the last frame block ends as high as that allows and has all slots live, both within the excerpt's token blocks. `band_width`: some head has band width 2.
All inputs are finite; a program needn't handle non-finite values.
Results may differ from the reference program's by a relative error of at most 0.0045.
The reference program's roundings to bfloat16 on the way count: a program that leaves them out, or rounds other values in their place, can miss the bound.
Values may be sent and summed in bfloat16 or wider, within the bound.
A program may use at most 192 MiB of HBM per device.

```python
import jax
import jax.numpy as jnp
from jax import lax

D = 1024
BANDED_ATTEND_CT = 16
MIXED_ATTEND_CNT = 8
HD = 64
CD = 512
LEVELS = 8
BLK = 128
WMAX = 2
TOKB = 48
RCH = 1
ALIST = 2
BPD = 4
QW = 1024
CQW = 512
TBD = 2
NBLK = 64
NTB = 32
FRAMES = 8192
TOKS = 1536


def alignment_pair(key):
    first_key, third_key = jax.random.split(jax.random.fold_in(key, 11), 2)
    blocks = jnp.arange(NBLK, dtype=jnp.int32)
    aligned = blocks * TBD // BPD
    lowest = jnp.maximum(-RCH, -aligned)
    upper_limit_value = jnp.minimum(RCH - ALIST + 1, NTB - ALIST - aligned)
    spread = jax.random.randint(first_key, (NBLK,), 0, 1000)
    offset = lowest + spread % (upper_limit_value - lowest + 1)
    first_of_device = blocks % BPD == 0
    last_of_device = blocks % BPD == BPD - 1
    offset = jnp.where(first_of_device, lowest, offset)
    offset = jnp.where(last_of_device, upper_limit_value, offset)
    lists = aligned[:, None] + offset[:, None] + jnp.arange(ALIST, dtype=jnp.int32)[None, :]
    live = jax.random.randint(third_key, (NBLK,), 1, ALIST + 1)
    live = jnp.where(last_of_device, ALIST, live)
    return (lists.astype(jnp.int32), live.astype(jnp.int32))


def draw_alignment(key, part):
    return alignment_pair(key)[0]


def draw_counts(key, part):
    return alignment_pair(key)[1]


def draw_band_width(key, part):
    first_key, second_key = jax.random.split(jax.random.fold_in(key, 23), 2)
    widths = jax.random.randint(first_key, (BANDED_ATTEND_CT,), 0, WMAX + 1)
    chosen = jax.random.randint(second_key, (), 0, BANDED_ATTEND_CT)
    return jnp.where(jnp.arange(BANDED_ATTEND_CT) == chosen, WMAX, widths).astype(jnp.int32)


def normalizer_heat_factors(key, attender_count):
    lowest, upper_limit_value = (0.5, 4.0)
    spread = jax.random.uniform(key, (attender_count,), jnp.float32, jnp.log(lowest), jnp.log(upper_limit_value))
    return jnp.exp(spread)


def draw_banded_attender_factor(key, part):
    return normalizer_heat_factors(jax.random.fold_in(key, 31), BANDED_ATTEND_CT)


def draw_cross_temp(key, part):
    return normalizer_heat_factors(jax.random.fold_in(key, 37), MIXED_ATTEND_CNT)


def touch_ends(array, key, least, top_value):
    dims = array.shape
    place = [jax.random.randint(jax.random.fold_in(key, axis), (), 0, dims[axis]) for axis in range(len(dims))]
    array = array.at[tuple(place)].set(least)
    longest = dims.index(max(dims))
    place[longest] = (place[longest] + 1) % dims[longest]
    return array.at[tuple(place)].set(top_value)


def block_scale(rng, extent, pieces, least, high):
    level = 1.0
    for axis_at, blocks in pieces:
        heights = jax.random.uniform(jax.random.fold_in(jax.random.fold_in(rng, 6), axis_at), (blocks,), jnp.float32, least / len(pieces), high / len(pieces))
        level = level * jnp.repeat(jnp.exp(heights), extent[axis_at] // blocks).reshape((-1,) + (1,) * (len(extent) - 1 - axis_at))
    return level


def noise(stream_key, dims, scale, most, pieces=(), kind=jnp.bfloat16):
    drawn = scale * jax.random.normal(stream_key, dims, jnp.float32)
    if pieces:
        drawn = drawn * block_scale(stream_key, dims, pieces, -0.22, 0.18)
    return jnp.clip(drawn, -most, most).astype(kind)


def setup_inputs(seed: int = 0, part: int = 0) -> dict:
    seeds = jax.random.split(jax.random.key(seed), 15)
    part_splits = jax.random.split(jax.random.fold_in(seeds[14], part), 15)
    return {
        "frames": noise(part_splits[0], (FRAMES, D), 1.0, 6.0, ((0, 16),)),
        "context": noise(part_splits[1], (TOKS, CD), 1.0, 6.0, ((0, 16),)),
        "noise_level": touch_ends(jax.random.randint(part_splits[2], (NBLK,), 0, LEVELS), jax.random.fold_in(part_splits[2], 1), 0, LEVELS - 1).astype(jnp.int32),
        "alignment": draw_alignment(jax.random.fold_in(jax.random.fold_in(seeds[14], part), 71), part),
        "counts": draw_counts(jax.random.fold_in(jax.random.fold_in(seeds[14], part), 71), part),
        "band_width": draw_band_width(jax.random.fold_in(seeds[14], 71), part),
        "mod_table": noise(seeds[6], (LEVELS, 2 * D), 0.5, 3.0, (), jnp.float32),
        "qkv_weight": noise(seeds[7], (D, 3 * QW), D ** -0.5, 0.1875),
        "out_weight": noise(seeds[8], (QW, D), QW ** -0.5, 0.1875),
        "cross_query_weight": noise(seeds[9], (D, CQW), D ** -0.5, 0.1875),
        "cross_kv_weight": noise(seeds[10], (CD, 2 * CQW), CD ** -0.5, 0.25),
        "cross_out_weight": noise(seeds[11], (CQW, D), CQW ** -0.5, 0.25),
        "banded_attender_factor": draw_banded_attender_factor(jax.random.fold_in(seeds[14], 71), part),
        "cross_temp": draw_cross_temp(jax.random.fold_in(seeds[14], 71), part),
    }


def head_norm(matrix, heads):
    count_rows = matrix.shape[0]
    parts = matrix.reshape(count_rows, heads, -1)
    parts = parts * lax.rsqrt(lax.optimization_barrier(jnp.mean(parts * parts, axis=-1, keepdims=True)) + 1e-06)
    return parts.reshape(count_rows, -1)

def masked_softmax(scores, allowed):
    scores = jnp.where(allowed, scores, -jnp.inf)
    peak = lax.optimization_barrier(jnp.max(scores, axis=-1, keepdims=True))
    powers = jnp.exp(scores - peak)
    return powers / lax.optimization_barrier(jnp.sum(powers, axis=-1, keepdims=True))

def reference(frames, context, noise_level, alignment, counts, band_width, mod_table, qkv_weight, out_weight, cross_query_weight, cross_kv_weight, cross_out_weight, banded_attender_factor, cross_temp):
    model_width = frames.shape[1]
    input_arrays = frames.astype(jnp.float32)
    normed = input_arrays * lax.rsqrt(lax.optimization_barrier(jnp.mean(input_arrays * input_arrays, axis=1, keepdims=True)) + 1e-06)
    modulation = mod_table[noise_level]
    hidden = (normed.reshape(NBLK, BLK, model_width) * (1.0 + modulation[:, None, :model_width]) + modulation[:, None, model_width:]).reshape(FRAMES, model_width).astype(jnp.bfloat16)
    projected = jnp.dot(hidden, qkv_weight, preferred_element_type=jnp.float32)
    queries = head_norm(projected[:, :QW], BANDED_ATTEND_CT).astype(jnp.bfloat16)
    keys_all = head_norm(projected[:, QW:2 * QW], BANDED_ATTEND_CT).astype(jnp.bfloat16)
    values_all = projected[:, 2 * QW:].astype(jnp.bfloat16)
    alignment_slack = WMAX * BLK
    lookup_vectors_padded = jnp.pad(keys_all, ((alignment_slack, alignment_slack), (0, 0)))
    values_pad = jnp.pad(values_all, ((alignment_slack, alignment_slack), (0, 0)))
    cross_queries = head_norm(jnp.dot(hidden, cross_query_weight, preferred_element_type=jnp.float32), MIXED_ATTEND_CNT).astype(jnp.bfloat16)
    cross_both = jnp.dot(context, cross_kv_weight, preferred_element_type=jnp.float32)
    cross_keys = head_norm(cross_both[:, :CQW], MIXED_ATTEND_CNT).astype(jnp.bfloat16)
    cross_values = cross_both[:, CQW:].astype(jnp.bfloat16)
    self_scale = banded_attender_factor * HD ** (-0.5)
    cross_scale = cross_temp * HD ** (-0.5)

    def one_block(block):
        first_row = block * BLK
        query_rows = lax.dynamic_slice_in_dim(queries, first_row, BLK, 0).astype(jnp.float32).reshape(BLK, BANDED_ATTEND_CT, HD)
        key_rows = lax.dynamic_slice_in_dim(lookup_vectors_padded, first_row, BLK + 2 * alignment_slack, 0).astype(jnp.float32).reshape(-1, BANDED_ATTEND_CT, HD)
        value_rows = lax.dynamic_slice_in_dim(values_pad, first_row, BLK + 2 * alignment_slack, 0).astype(jnp.float32).reshape(-1, BANDED_ATTEND_CT, HD)
        key_block = block - WMAX + jnp.arange(BLK + 2 * alignment_slack, dtype=jnp.int32) // BLK
        within_band_flag = (jnp.abs(block - key_block)[None, None, :] <= band_width[:, None, None]) & ((key_block >= 0) & (key_block < NBLK))[None, None, :]
        scores = jnp.einsum('ihd,jhd->hij', query_rows, key_rows) * self_scale[:, None, None]
        weights = lax.optimization_barrier(masked_softmax(scores, within_band_flag).astype(jnp.bfloat16)).astype(jnp.float32)
        self_out = jnp.einsum('hij,jhd->ihd', weights, value_rows).reshape(BLK, QW).astype(jnp.bfloat16)
        picked_keys = jnp.concatenate([lax.dynamic_slice_in_dim(cross_keys, (alignment[block, slot] * TOKB).astype(jnp.int32), TOKB, 0) for slot in range(ALIST)], 0)
        picked_values = jnp.concatenate([lax.dynamic_slice_in_dim(cross_values, (alignment[block, slot] * TOKB).astype(jnp.int32), TOKB, 0) for slot in range(ALIST)], 0)
        live = jnp.repeat(jnp.arange(ALIST, dtype=jnp.int32) < counts[block], TOKB)
        cross_rows = lax.dynamic_slice_in_dim(cross_queries, first_row, BLK, 0).astype(jnp.float32).reshape(BLK, MIXED_ATTEND_CNT, HD)
        cross_scores = jnp.einsum('ihd,jhd->hij', cross_rows, picked_keys.astype(jnp.float32).reshape(-1, MIXED_ATTEND_CNT, HD)) * cross_scale[:, None, None]
        cross_weights = lax.optimization_barrier(masked_softmax(cross_scores, live[None, None, :]).astype(jnp.bfloat16)).astype(jnp.float32)
        cross_out = jnp.einsum('hij,jhd->ihd', cross_weights, picked_values.astype(jnp.float32).reshape(-1, MIXED_ATTEND_CNT, HD)).reshape(BLK, CQW).astype(jnp.bfloat16)
        return (self_out, cross_out)
    self_all, cross_all = lax.map(one_block, jnp.arange(NBLK, dtype=jnp.int32))
    self_all = self_all.reshape(FRAMES, QW)
    cross_all = cross_all.reshape(FRAMES, CQW)
    total = jnp.dot(self_all, out_weight, preferred_element_type=jnp.float32) + jnp.dot(cross_all, cross_out_weight, preferred_element_type=jnp.float32)
    return total.astype(jnp.bfloat16)
```

```python
import functools
import math

import jax
import jax.numpy as jnp
from jax import lax
from jax.experimental import pallas as pl
from jax.experimental.pallas import tpu as pltpu
from jax.sharding import PartitionSpec as P

BANDED_ATTEND_CT = 16
MIXED_ATTEND_CNT = 8
HD = 64
LEVELS = 8
BLK = 128
WMAX = 2
TOKB = 48
RCH = 1
ALIST = 2
PAIR = 2 * HD
HALO = WMAX * BLK
CHUNK = 256
EPS = 1e-06
SAFE_FACTOR = 6.0
MESH = pl.DeviceIdType.MESH


def pair_norm(part):
    low = lax.broadcasted_iota(jnp.int32, part.shape, 1) < HD
    square = part * part
    first = jnp.sum(jnp.where(low, square, 0.0), axis=-1, keepdims=True)
    second = jnp.sum(jnp.where(low, 0.0, square), axis=-1, keepdims=True)
    mean = jnp.where(low, first, second) * (1.0 / HD)
    return part * lax.rsqrt(mean + EPS)


def project_kernel(
    devices,
    frames,
    context,
    noise,
    mod,
    wqkv,
    wcq,
    wckv,
    q_out,
    k_out,
    v_out,
    cq_out,
    ck_out,
    cv_out,
    window,
    tokens,
    noise_halo,
    hidden,
    wqkv_v,
    wcq_v,
    wckv_v,
    local_sem,
    weight_sem,
    send_sem,
    recv_sem,
):
    me = lax.axis_index("seq")
    rows, width = frames.shape
    blocks = rows // BLK
    token_rows = context.shape[0]
    margin = RCH * TOKB
    qw = q_out.shape[1]
    cw = cq_out.shape[1]
    has = (me > 0, me < devices - 1)

    fetch_frames = pltpu.make_async_copy(
        frames, window.at[pl.ds(HALO, rows), :], local_sem.at[0]
    )
    fetch_tokens = pltpu.make_async_copy(
        context, tokens.at[pl.ds(margin, token_rows), :], local_sem.at[1]
    )
    fetch_frames.start()
    weight_order = (1, 2, 0)
    fetch_w = {}
    for slot in weight_order:
        cols = pl.ds(slot * qw, qw)
        fetch_w[slot] = pltpu.make_async_copy(
            wqkv.at[:, cols], wqkv_v.at[:, cols], weight_sem.at[slot]
        )
        fetch_w[slot].start()
    fetch_cq = pltpu.make_async_copy(wcq, wcq_v, weight_sem.at[3])
    fetch_ckv = pltpu.make_async_copy(wckv, wckv_v, weight_sem.at[4])

    barrier = pltpu.get_barrier_semaphore()
    for side in (0, 1):

        @pl.when(has[side])
        def _(side=side):
            pl.semaphore_signal(
                barrier, inc=1, device_id={"seq": me + 2 * side - 1}, device_id_type=MESH
            )

    peers = jnp.minimum(me, 1) + jnp.minimum(devices - 1 - me, 1)
    pl.semaphore_wait(barrier, peers)

    def copies(side):
        other = 1 - side
        peer = {"seq": me + 2 * side - 1}
        edge = rows - HALO if side else 0
        land = 0 if side else HALO + rows
        token_edge = token_rows - margin if side else 0
        token_land = 0 if side else margin + token_rows
        triples = (
            (noise, noise_halo.at[other]),
            (frames.at[pl.ds(edge, HALO), :], window.at[pl.ds(land, HALO), :]),
            (
                context.at[pl.ds(token_edge, margin), :],
                tokens.at[pl.ds(token_land, margin), :],
            ),
        )
        return [
            pltpu.make_async_remote_copy(
                src_ref=source,
                dst_ref=target,
                send_sem=send_sem.at[side, index],
                recv_sem=recv_sem.at[other, index],
                device_id=peer,
                device_id_type=MESH,
            )
            for index, (source, target) in enumerate(triples)
        ]

    sends = [copies(0), copies(1)]
    for side in (0, 1):

        @pl.when(has[side])
        def _(side=side):
            for copy in sends[side]:
                copy.start()

    fetch_cq.start()
    fetch_ckv.start()
    fetch_tokens.start()

    def make_hidden(row, level):
        scale = jnp.zeros((1, width), jnp.float32)
        shift = jnp.zeros((1, width), jnp.float32)
        for entry in range(LEVELS):
            here = level == entry
            scale = jnp.where(here, mod[entry : entry + 1, :width], scale)
            shift = jnp.where(here, mod[entry : entry + 1, width:], shift)
        place = pl.ds(pl.multiple_of(row, BLK), BLK)
        values = window[place, :].astype(jnp.float32)
        mean = jnp.mean(values * values, axis=1, keepdims=True)
        normed = values * lax.rsqrt(mean + EPS)
        hidden[place, :] = (normed * (1.0 + scale) + shift).astype(jnp.bfloat16)

    def project(source, place, weight, first_col, target, normalize):
        total = target.shape[1]

        def step(index, carry):
            out_cols = pl.multiple_of(index * CHUNK, CHUNK)
            y = jnp.dot(
                source[place, :],
                weight[:, pl.ds(pl.multiple_of(first_col + index * CHUNK, CHUNK), CHUNK)],
                preferred_element_type=jnp.float32,
            )
            for part in range(CHUNK // PAIR):
                piece = y[:, part * PAIR : (part + 1) * PAIR]
                if normalize:
                    piece = pair_norm(piece)
                target[place_of(target, place), pl.ds(out_cols + part * PAIR, PAIR)] = (
                    piece.astype(jnp.bfloat16)
                )
            return carry

        lax.fori_loop(0, total // CHUNK, step, 0)

    def place_of(target, place):
        if target.shape[0] == rows:
            return pl.ds(0, rows)
        return place

    fetch_frames.wait()
    for block in range(blocks):
        make_hidden(HALO + block * BLK, noise[:, block : block + 1])
    local = pl.ds(HALO, rows)
    fetch_w[1].wait()
    project(hidden, local, wqkv_v, qw, k_out, True)
    fetch_w[2].wait()
    project(hidden, local, wqkv_v, 2 * qw, v_out, False)
    fetch_w[0].wait()
    project(hidden, local, wqkv_v, 0, q_out, True)
    fetch_cq.wait()
    project(hidden, local, wcq_v, 0, cq_out, True)

    fetch_ckv.wait()
    fetch_tokens.wait()

    def halo_step(step, carry):
        side = lax.rem(me + 1 + step, 2)
        present = jnp.where(side == 0, me > 0, me < devices - 1)
        row = pl.multiple_of(side * (HALO + rows), BLK)
        token_row = pl.multiple_of(side * (margin + token_rows), 16)

        @pl.when(present)
        def _():
            waits = (
                noise_halo.at[0],
                window.at[pl.ds(0, HALO), :],
                tokens.at[pl.ds(0, margin), :],
            )
            for index, ref in enumerate(waits):
                pltpu.make_async_copy(ref, ref, recv_sem.at[side, index]).wait()
            levels = noise_halo[side]
            for block in range(WMAX):
                low_side = levels[:, blocks - WMAX + block : blocks - WMAX + block + 1]
                level = jnp.where(side == 0, low_side, levels[:, block : block + 1])
                make_hidden(row + block * BLK, level)

        @pl.when(jnp.logical_not(present))
        def _():
            hidden[pl.ds(row, HALO), :] = jnp.zeros((HALO, width), jnp.bfloat16)
            tokens[pl.ds(token_row, margin), :] = jnp.zeros(
                (margin, tokens.shape[1]), jnp.bfloat16
            )

        place = pl.ds(row, HALO)
        project(hidden, place, wqkv_v, qw, k_out, True)
        project(hidden, place, wqkv_v, 2 * qw, v_out, False)
        return carry

    lax.fori_loop(0, 2, halo_step, 0)
    every = pl.ds(0, tokens.shape[0])
    project(tokens, every, wckv_v, 0, ck_out, True)
    project(tokens, every, wckv_v, cw, cv_out, False)

    for side in (0, 1):

        @pl.when(has[side])
        def _(side=side):
            for copy in sends[side]:
                copy.wait_send()


def attend_kernel(
    devices,
    me_ref,
    band,
    factor,
    temp,
    alignment,
    counts,
    q,
    k,
    v,
    cq,
    ck,
    cv,
    wo,
    wco,
    out,
    values,
    acc,
    self_out,
    cross_out,
    wo_v,
    wco_v,
    sem,
):
    me = me_ref[0]
    rows = q.shape[0]
    blocks = rows // BLK
    window_rows = k.shape[0]
    span = ALIST * TOKB
    fetch_wo = pltpu.make_async_copy(wo, wo_v, sem.at[0])
    fetch_wco = pltpu.make_async_copy(wco, wco_v, sem.at[1])
    fetch_wo.start()
    fetch_wco.start()
    to_base2 = HD ** (-0.5) * math.log2(math.e)

    def half(shape, parity):
        lane = lax.broadcasted_iota(jnp.int32, shape, 1)
        return (lane < HD) if parity == 0 else (lane >= HD)

    def scores_of(query, key):
        return lax.dot_general(
            query, key, (((1,), (1,)), ((), ())), preferred_element_type=jnp.float32
        )

    def shifted_powers(scores, allowed):
        scores = jnp.where(allowed, scores, -jnp.inf)
        return jnp.exp2(scores - jnp.max(scores, axis=-1, keepdims=True))

    def combine(target, cols):
        for block in range(blocks):
            place = pl.ds(block * BLK, BLK)
            first = acc[0, place, :]
            second = acc[1, place, :]
            low = half(first.shape, 0)
            total = pltpu.roll(jnp.where(low, second, first), HD, 1)
            target[place, cols] = (jnp.where(low, first, second) / total).astype(jnp.bfloat16)

    def self_pair(pair, carry):
        cols = pl.ds(pl.multiple_of(pair * PAIR, PAIR), PAIR)
        for parity in (0, 1):
            head = 2 * pair + parity
            reach = band[head]
            scale = factor[head] * to_base2
            safe = factor[head] <= SAFE_FACTOR
            row_block = (
                lax.broadcasted_iota(jnp.int32, (window_rows, PAIR), 0) // BLK
                + me * blocks
                - WMAX
            )
            valid = (row_block >= 0) & (row_block < devices * blocks)
            ones = jnp.where(valid, 1.0, 0.0).astype(jnp.bfloat16)
            values[parity] = jnp.where(half((window_rows, PAIR), parity), v[:, cols], ones)
            for size in range(WMAX + 1):

                @pl.when(safe & (reach == size))
                def _(size=size, parity=parity):
                    for block in range(blocks):
                        query = q[pl.ds(block * BLK, BLK), cols]
                        query = jnp.where(half(query.shape, parity), query, jnp.zeros_like(query))
                        keys = pl.ds((block + WMAX - size) * BLK, (2 * size + 1) * BLK)
                        powers = jnp.exp2(scores_of(query, k[keys, cols]) * scale)
                        acc[parity, pl.ds(block * BLK, BLK), :] = jnp.dot(
                            powers.astype(jnp.bfloat16),
                            values[parity, keys, :],
                            preferred_element_type=jnp.float32,
                        )

            @pl.when(jnp.logical_not(safe))
            def _(parity=parity):
                def one(block, inner):
                    first = pl.multiple_of(block * BLK, BLK)
                    query = q[pl.ds(first, BLK), cols]
                    query = jnp.where(half(query.shape, parity), query, jnp.zeros_like(query))
                    keys = pl.ds(first, (2 * WMAX + 1) * BLK)
                    scores = scores_of(query, k[keys, cols]) * scale
                    offset = lax.broadcasted_iota(jnp.int32, scores.shape, 1) // BLK - WMAX
                    key_block = offset + block + me * blocks
                    allowed = (
                        (jnp.abs(offset) <= reach)
                        & (key_block >= 0)
                        & (key_block < devices * blocks)
                    )
                    acc[parity, pl.ds(first, BLK), :] = jnp.dot(
                        shifted_powers(scores, allowed).astype(jnp.bfloat16),
                        values[parity, keys, :],
                        preferred_element_type=jnp.float32,
                    )
                    return inner

                lax.fori_loop(0, blocks, one, 0)

        combine(self_out, cols)
        return carry

    lax.fori_loop(0, BANDED_ATTEND_CT // 2, self_pair, 0)

    token_blocks = ck.shape[0] // TOKB - 2 * RCH

    def cross_pair(pair, carry):
        cols = pl.ds(pl.multiple_of(pair * PAIR, PAIR), PAIR)
        for parity in (0, 1):
            head = 2 * pair + parity
            scale = temp[head] * to_base2
            safe = temp[head] <= SAFE_FACTOR

            def run(shifted, parity=parity, scale=scale):
                for block in range(blocks):
                    lowest = jnp.minimum(alignment[block, 0], alignment[block, 1])
                    live = counts[block]
                    admit = [
                        jnp.where(
                            ((alignment[block, 0] == lowest + slot) & (live > 0))
                            | ((alignment[block, 1] == lowest + slot) & (live > 1)),
                            1,
                            0,
                        )
                        for slot in range(ALIST)
                    ]
                    start = (lowest - (me * token_blocks - RCH)) * TOKB
                    place = pl.ds(pl.multiple_of(start, 16), span)
                    query = cq[pl.ds(block * BLK, BLK), cols]
                    query = jnp.where(half(query.shape, parity), query, jnp.zeros_like(query))
                    scores = scores_of(query, ck[place, cols]) * scale
                    row = lax.broadcasted_iota(jnp.int32, (span, PAIR), 0)
                    row_ok = jnp.where(row < TOKB, admit[0], admit[1]) > 0
                    value = jnp.where(
                        half((span, PAIR), parity),
                        cv[place, cols],
                        jnp.ones((span, PAIR), jnp.bfloat16),
                    )
                    value = jnp.where(row_ok, value, jnp.zeros_like(value))
                    if shifted:
                        token = lax.broadcasted_iota(jnp.int32, scores.shape, 1)
                        ok = jnp.where(token < TOKB, admit[0], admit[1]) > 0
                        powers = shifted_powers(scores, ok)
                    else:
                        powers = jnp.exp2(scores)
                    acc[parity, pl.ds(block * BLK, BLK), :] = jnp.dot(
                        powers.astype(jnp.bfloat16), value, preferred_element_type=jnp.float32
                    )

            pl.when(safe)(functools.partial(run, False))
            pl.when(jnp.logical_not(safe))(functools.partial(run, True))
        combine(cross_out, cols)
        return carry

    lax.fori_loop(0, MIXED_ATTEND_CNT // 2, cross_pair, 0)
    fetch_wo.wait()
    fetch_wco.wait()

    def finish(index, carry):
        cols = pl.ds(pl.multiple_of(index * CHUNK, CHUNK), CHUNK)
        total = jnp.dot(self_out[...], wo_v[:, cols], preferred_element_type=jnp.float32)
        total += jnp.dot(cross_out[...], wco_v[:, cols], preferred_element_type=jnp.float32)
        out[:, cols] = total.astype(jnp.bfloat16)
        return carry

    lax.fori_loop(0, out.shape[1] // CHUNK, finish, 0)


def shards(
    frames,
    context,
    noise_level,
    alignment,
    counts,
    band_width,
    mod_table,
    qkv_weight,
    out_weight,
    cross_query_weight,
    cross_kv_weight,
    cross_out_weight,
    banded_attender_factor,
    cross_temp,
):
    rows, width = frames.shape
    blocks = rows // BLK
    qw = qkv_weight.shape[1] // 3
    cw = cross_query_weight.shape[1]
    devices = lax.axis_size("seq")
    window_rows = rows + 2 * HALO
    token_rows = context.shape[0] + 2 * RCH * TOKB
    bf16 = jnp.bfloat16
    any_spec = pl.BlockSpec(memory_space=pl.ANY)
    vmem = pl.BlockSpec(memory_space=pltpu.VMEM)
    smem = pl.BlockSpec(memory_space=pltpu.SMEM)
    shapes = [
        (rows, qw),
        (window_rows, qw),
        (window_rows, qw),
        (rows, cw),
        (token_rows, cw),
        (token_rows, cw),
    ]
    projected = pl.pallas_call(
        functools.partial(project_kernel, devices),
        out_shape=[jax.ShapeDtypeStruct(shape, bf16) for shape in shapes],
        in_specs=[any_spec, any_spec, vmem, vmem, any_spec, any_spec, any_spec],
        out_specs=[vmem] * 6,
        scratch_shapes=[
            pltpu.VMEM((window_rows, width), bf16),
            pltpu.VMEM((token_rows, context.shape[1]), bf16),
            pltpu.VMEM((2, 1, blocks), jnp.int32),
            pltpu.VMEM((window_rows, width), bf16),
            pltpu.VMEM(qkv_weight.shape, bf16),
            pltpu.VMEM(cross_query_weight.shape, bf16),
            pltpu.VMEM(cross_kv_weight.shape, bf16),
            pltpu.SemaphoreType.DMA((2,)),
            pltpu.SemaphoreType.DMA((5,)),
            pltpu.SemaphoreType.DMA((2, 3)),
            pltpu.SemaphoreType.DMA((2, 3)),
        ],
        compiler_params=pltpu.CompilerParams(collective_id=0, has_side_effects=True),
        name="project",
    )(
        frames,
        context,
        noise_level.reshape(1, blocks),
        mod_table,
        qkv_weight,
        cross_query_weight,
        cross_kv_weight,
    )
    me = lax.axis_index("seq").astype(jnp.int32).reshape(1)
    return pl.pallas_call(
        functools.partial(attend_kernel, devices),
        out_shape=jax.ShapeDtypeStruct((rows, width), bf16),
        in_specs=[smem] * 6 + [vmem] * 6 + [any_spec] * 2,
        out_specs=vmem,
        scratch_shapes=[
            pltpu.VMEM((2, window_rows, PAIR), bf16),
            pltpu.VMEM((2, rows, PAIR), jnp.float32),
            pltpu.VMEM((rows, qw), bf16),
            pltpu.VMEM((rows, cw), bf16),
            pltpu.VMEM(out_weight.shape, bf16),
            pltpu.VMEM(cross_out_weight.shape, bf16),
            pltpu.SemaphoreType.DMA((2,)),
        ],
        name="attend",
    )(
        me,
        band_width,
        banded_attender_factor,
        cross_temp,
        alignment,
        counts,
        *projected,
        out_weight,
        cross_out_weight,
    )


def solution(mesh):
    placed = (
        P(("groups", "seq"), None),
        P(("groups", "seq"), None),
        P(("groups", "seq")),
        P(("groups", "seq"), None),
        P(("groups", "seq")),
        P(),
        P(),
        P(),
        P(),
        P(),
        P(),
        P(),
        P(),
        P(),
    )
    return jax.shard_map(
        shards, mesh=mesh, in_specs=placed, out_specs=P(("groups", "seq"), None), check_vma=False
    )
```

```python
import functools
import math

import jax
import jax.numpy as jnp
from jax import lax
from jax.experimental import pallas as pl
from jax.experimental.pallas import tpu as pltpu
from jax.sharding import PartitionSpec as P

BANDED_ATTEND_CT = 16
MIXED_ATTEND_CNT = 8
HD = 64
LEVELS = 8
BLK = 128
WMAX = 2
TOKB = 48
RCH = 1
ALIST = 2
PAIR = 2 * HD
HALO = WMAX * BLK
CHUNK = 256
SLAB = 32
EPS = 1e-06
VMEM_LIMIT = 32 * 1024 * 1024
PROJECT_VMEM = 54 * 1024 * 1024
SAFE_FACTOR = 6.0
MESH = pl.DeviceIdType.MESH


def pair_norm(part):
    low = lax.broadcasted_iota(jnp.int32, part.shape, 1) < HD
    square = part * part
    first = jnp.sum(jnp.where(low, square, 0.0), axis=-1, keepdims=True)
    second = jnp.sum(jnp.where(low, 0.0, square), axis=-1, keepdims=True)
    mean = jnp.where(low, first, second) * (1.0 / HD)
    return part * lax.rsqrt(mean + EPS)


def project_kernel(
    devices,
    frames,
    context,
    noise,
    mod,
    wqkv,
    wcq,
    wckv,
    q_out,
    k_out,
    v_out,
    cq_out,
    ck_out,
    cv_out,
    window,
    tokens,
    noise_halo,
    hidden,
    wqkv_v,
    wcq_v,
    wckv_v,
    local_sem,
    weight_sem,
    send_sem,
    recv_sem,
):
    me = lax.axis_index("seq")
    rows, width = frames.shape
    blocks = rows // BLK
    token_rows = context.shape[0]
    margin = RCH * TOKB
    qw = q_out.shape[1]
    cw = cq_out.shape[1]
    has = (me > 0, me < devices - 1)

    fetch_frames = pltpu.make_async_copy(
        frames, window.at[pl.ds(HALO, rows), :], local_sem.at[0]
    )
    fetch_tokens = pltpu.make_async_copy(
        context, tokens.at[pl.ds(margin, token_rows), :], local_sem.at[1]
    )
    fetch_frames.start()
    weight_order = (1, 2, 0)
    fetch_w = {}
    for slot in weight_order:
        cols = pl.ds(slot * qw, qw)
        fetch_w[slot] = pltpu.make_async_copy(
            wqkv.at[:, cols], wqkv_v.at[:, cols], weight_sem.at[slot]
        )
        fetch_w[slot].start()
    fetch_cq = pltpu.make_async_copy(wcq, wcq_v, weight_sem.at[3])
    fetch_ckv = pltpu.make_async_copy(wckv, wckv_v, weight_sem.at[4])

    barrier = pltpu.get_barrier_semaphore()
    for side in (0, 1):

        @pl.when(has[side])
        def _(side=side):
            pl.semaphore_signal(
                barrier, inc=1, device_id={"seq": me + 2 * side - 1}, device_id_type=MESH
            )

    peers = jnp.minimum(me, 1) + jnp.minimum(devices - 1 - me, 1)
    pl.semaphore_wait(barrier, peers)

    def copies(side):
        other = 1 - side
        peer = {"seq": me + 2 * side - 1}
        edge = rows - HALO if side else 0
        land = 0 if side else HALO + rows
        token_edge = token_rows - margin if side else 0
        token_land = 0 if side else margin + token_rows
        triples = (
            (noise, noise_halo.at[other]),
            (frames.at[pl.ds(edge, HALO), :], window.at[pl.ds(land, HALO), :]),
            (
                context.at[pl.ds(token_edge, margin), :],
                tokens.at[pl.ds(token_land, margin), :],
            ),
        )
        return [
            pltpu.make_async_remote_copy(
                src_ref=source,
                dst_ref=target,
                send_sem=send_sem.at[side, index],
                recv_sem=recv_sem.at[other, index],
                device_id=peer,
                device_id_type=MESH,
            )
            for index, (source, target) in enumerate(triples)
        ]

    sends = [copies(0), copies(1)]
    for side in (0, 1):

        @pl.when(has[side])
        def _(side=side):
            for copy in sends[side]:
                copy.start()

    fetch_cq.start()
    fetch_ckv.start()
    fetch_tokens.start()

    def make_hidden(row, level):
        scale = jnp.zeros((1, width), jnp.float32)
        shift = jnp.zeros((1, width), jnp.float32)
        for entry in range(LEVELS):
            here = level == entry
            scale = jnp.where(here, mod[entry : entry + 1, :width], scale)
            shift = jnp.where(here, mod[entry : entry + 1, width:], shift)
        for slab in range(BLK // SLAB):
            place = pl.ds(pl.multiple_of(row + slab * SLAB, SLAB), SLAB)
            values = window[place, :].astype(jnp.float32)
            mean = jnp.mean(values * values, axis=1, keepdims=True)
            normed = values * lax.rsqrt(mean + EPS)
            hidden[place, :] = (normed * (1.0 + scale) + shift).astype(jnp.bfloat16)

    def project(source, place, jobs):
        total = jobs[0][3].shape[1]

        def step(index, carry):
            out_cols = pl.multiple_of(index * CHUNK, CHUNK)
            for target_place, weight, first_col, target, normalize in jobs:
                y = jnp.dot(
                    source[place, :],
                    weight[:, pl.ds(pl.multiple_of(first_col + index * CHUNK, CHUNK), CHUNK)],
                    preferred_element_type=jnp.float32,
                )
                for part in range(CHUNK // PAIR):
                    piece = y[:, part * PAIR : (part + 1) * PAIR]
                    if normalize:
                        piece = pair_norm(piece)
                    target[target_place, pl.ds(out_cols + part * PAIR, PAIR)] = piece.astype(
                        jnp.bfloat16
                    )
            return carry

        lax.fori_loop(0, total // CHUNK, step, 0)

    fetch_frames.wait()
    for block in range(blocks):
        make_hidden(HALO + block * BLK, noise[:, block : block + 1])
    local = pl.ds(HALO, rows)
    for slot in weight_order:
        fetch_w[slot].wait()
    inner = pl.ds(0, rows)
    project(
        hidden,
        local,
        (
            (local, wqkv_v, qw, k_out, True),
            (local, wqkv_v, 2 * qw, v_out, False),
            (inner, wqkv_v, 0, q_out, True),
        ),
    )
    fetch_cq.wait()
    project(hidden, local, ((inner, wcq_v, 0, cq_out, True),))

    fetch_ckv.wait()
    fetch_tokens.wait()

    def halo_step(step, carry):
        side = lax.rem(me + 1 + step, 2)
        present = jnp.where(side == 0, me > 0, me < devices - 1)
        row = pl.multiple_of(side * (HALO + rows), BLK)
        token_row = pl.multiple_of(side * (margin + token_rows), 16)

        @pl.when(present)
        def _():
            waits = (
                noise_halo.at[0],
                window.at[pl.ds(0, HALO), :],
                tokens.at[pl.ds(0, margin), :],
            )
            for index, ref in enumerate(waits):
                pltpu.make_async_copy(ref, ref, recv_sem.at[side, index]).wait()
            levels = noise_halo[side]
            for block in range(WMAX):
                low_side = levels[:, blocks - WMAX + block : blocks - WMAX + block + 1]
                level = jnp.where(side == 0, low_side, levels[:, block : block + 1])
                make_hidden(row + block * BLK, level)

        @pl.when(jnp.logical_not(present))
        def _():
            hidden[pl.ds(row, HALO), :] = jnp.zeros((HALO, width), jnp.bfloat16)
            tokens[pl.ds(token_row, margin), :] = jnp.zeros(
                (margin, tokens.shape[1]), jnp.bfloat16
            )

        place = pl.ds(row, HALO)
        project(
            hidden,
            place,
            ((place, wqkv_v, qw, k_out, True), (place, wqkv_v, 2 * qw, v_out, False)),
        )
        return carry

    lax.fori_loop(0, 2, halo_step, 0)
    every = pl.ds(0, tokens.shape[0])
    project(
        tokens,
        every,
        ((every, wckv_v, 0, ck_out, True), (every, wckv_v, cw, cv_out, False)),
    )

    for side in (0, 1):

        @pl.when(has[side])
        def _(side=side):
            for copy in sends[side]:
                copy.wait_send()


def attend_kernel(
    devices,
    me_ref,
    band,
    factor,
    temp,
    alignment,
    counts,
    q,
    k,
    v,
    cq,
    ck,
    cv,
    wo,
    wco,
    out,
    ones,
    self_out,
    cross_out,
):
    me = me_ref[0]
    rows = q.shape[0]
    blocks = rows // BLK
    window_rows = k.shape[0]
    span = ALIST * TOKB
    to_base2 = HD ** (-0.5) * math.log2(math.e)

    def half(shape, parity):
        lane = lax.broadcasted_iota(jnp.int32, shape, 1)
        return (lane < HD) if parity == 0 else (lane >= HD)

    def scores_of(query, key):
        return lax.dot_general(
            query, key, (((1,), (1,)), ((), ())), preferred_element_type=jnp.float32
        )

    def shifted_powers(scores, allowed):
        scores = jnp.where(allowed, scores, -jnp.inf)
        return jnp.exp2(scores - jnp.max(scores, axis=-1, keepdims=True))

    row_block = (
        lax.broadcasted_iota(jnp.int32, (window_rows, PAIR), 0) // BLK + me * blocks - WMAX
    )
    valid = (row_block >= 0) & (row_block < devices * blocks)
    ones[...] = jnp.where(valid, 1.0, 0.0).astype(jnp.bfloat16)

    def half_query(source, block, cols, parity):
        query = source[pl.ds(block * BLK, BLK), cols]
        return jnp.where(half(query.shape, parity), query, jnp.zeros_like(query))

    def merge(first, second):
        low = half(first.shape, 0)
        total = pltpu.roll(jnp.where(low, second, first), HD, 1)
        return (jnp.where(low, first, second) / total).astype(jnp.bfloat16)

    def self_pair(pair, carry):
        cols = pl.ds(pl.multiple_of(pair * PAIR, PAIR), PAIR)
        reaches = [band[2 * pair + parity] for parity in (0, 1)]
        scales = [factor[2 * pair + parity] * to_base2 for parity in (0, 1)]
        safe = (factor[2 * pair] <= SAFE_FACTOR) & (factor[2 * pair + 1] <= SAFE_FACTOR)

        def fast(sizes):
            for block in range(blocks):
                sums = []
                for parity in (0, 1):
                    size = sizes[parity]
                    keys = pl.ds((block + WMAX - size) * BLK, (2 * size + 1) * BLK)
                    query = half_query(q, block, cols, parity)
                    value = v[keys, cols]
                    value = jnp.where(half(value.shape, parity), value, ones[keys, :])
                    powers = jnp.exp2(scores_of(query, k[keys, cols]) * scales[parity])
                    sums.append(
                        jnp.dot(
                            powers.astype(jnp.bfloat16), value, preferred_element_type=jnp.float32
                        )
                    )
                self_out[pl.ds(block * BLK, BLK), cols] = merge(*sums)

        for low_size in range(WMAX + 1):
            for high_size in range(WMAX + 1):
                pl.when(safe & (reaches[0] == low_size) & (reaches[1] == high_size))(
                    functools.partial(fast, (low_size, high_size))
                )

        @pl.when(jnp.logical_not(safe))
        def _():
            def one(block, inner):
                first = pl.multiple_of(block * BLK, BLK)
                keys = pl.ds(first, (2 * WMAX + 1) * BLK)
                sums = []
                for parity in (0, 1):
                    query = q[pl.ds(first, BLK), cols]
                    query = jnp.where(half(query.shape, parity), query, jnp.zeros_like(query))
                    scores = scores_of(query, k[keys, cols]) * scales[parity]
                    offset = lax.broadcasted_iota(jnp.int32, scores.shape, 1) // BLK - WMAX
                    key_block = offset + block + me * blocks
                    allowed = (
                        (jnp.abs(offset) <= reaches[parity])
                        & (key_block >= 0)
                        & (key_block < devices * blocks)
                    )
                    value = v[keys, cols]
                    value = jnp.where(half(value.shape, parity), value, ones[keys, :])
                    sums.append(
                        jnp.dot(
                            shifted_powers(scores, allowed).astype(jnp.bfloat16),
                            value,
                            preferred_element_type=jnp.float32,
                        )
                    )
                self_out[pl.ds(first, BLK), cols] = merge(*sums)
                return inner

            lax.fori_loop(0, blocks, one, 0)

        return carry

    lax.fori_loop(0, BANDED_ATTEND_CT // 2, self_pair, 0)

    token_blocks = ck.shape[0] // TOKB - 2 * RCH

    def cross_pair(pair, carry):
        cols = pl.ds(pl.multiple_of(pair * PAIR, PAIR), PAIR)
        scales = [temp[2 * pair + parity] * to_base2 for parity in (0, 1)]
        safe = (temp[2 * pair] <= SAFE_FACTOR) & (temp[2 * pair + 1] <= SAFE_FACTOR)

        def run(shifted):
            for block in range(blocks):
                listed = [alignment[slot, block] for slot in range(ALIST)]
                lowest = jnp.minimum(listed[0], listed[1])
                live = counts[block]
                admit = [
                    jnp.where(
                        ((listed[0] == lowest + slot) & (live > 0))
                        | ((listed[1] == lowest + slot) & (live > 1)),
                        1,
                        0,
                    )
                    for slot in range(ALIST)
                ]
                start = (lowest - (me * token_blocks - RCH)) * TOKB
                place = pl.ds(pl.multiple_of(start, 16), span)
                row = lax.broadcasted_iota(jnp.int32, (span, PAIR), 0)
                row_ok = jnp.where(row < TOKB, admit[0], admit[1]) > 0
                sums = []
                for parity in (0, 1):
                    query = half_query(cq, block, cols, parity)
                    scores = scores_of(query, ck[place, cols]) * scales[parity]
                    value = cv[place, cols]
                    value = jnp.where(half(value.shape, parity), value, jnp.ones_like(value))
                    value = jnp.where(row_ok, value, jnp.zeros_like(value))
                    if shifted:
                        token = lax.broadcasted_iota(jnp.int32, scores.shape, 1)
                        ok = jnp.where(token < TOKB, admit[0], admit[1]) > 0
                        powers = shifted_powers(scores, ok)
                    else:
                        powers = jnp.exp2(scores)
                    sums.append(
                        jnp.dot(
                            powers.astype(jnp.bfloat16), value, preferred_element_type=jnp.float32
                        )
                    )
                cross_out[pl.ds(block * BLK, BLK), cols] = merge(*sums)

        pl.when(safe)(functools.partial(run, False))
        pl.when(jnp.logical_not(safe))(functools.partial(run, True))
        return carry

    lax.fori_loop(0, MIXED_ATTEND_CNT // 2, cross_pair, 0)
    def finish(index, carry):
        cols = pl.ds(pl.multiple_of(index * CHUNK, CHUNK), CHUNK)
        total = jnp.dot(self_out[...], wo[:, cols], preferred_element_type=jnp.float32)
        total += jnp.dot(cross_out[...], wco[:, cols], preferred_element_type=jnp.float32)
        out[:, cols] = total.astype(jnp.bfloat16)
        return carry

    lax.fori_loop(0, out.shape[1] // CHUNK, finish, 0)


def shards(
    frames,
    context,
    noise_level,
    alignment,
    counts,
    band_width,
    mod_table,
    qkv_weight,
    out_weight,
    cross_query_weight,
    cross_kv_weight,
    cross_out_weight,
    banded_attender_factor,
    cross_temp,
):
    rows, width = frames.shape
    blocks = rows // BLK
    qw = qkv_weight.shape[1] // 3
    cw = cross_query_weight.shape[1]
    devices = lax.axis_size("seq")
    window_rows = rows + 2 * HALO
    token_rows = context.shape[0] + 2 * RCH * TOKB
    bf16 = jnp.bfloat16
    hbm = pl.BlockSpec(memory_space=pltpu.HBM)
    vmem = pl.BlockSpec(memory_space=pltpu.VMEM)
    smem = pl.BlockSpec(memory_space=pltpu.SMEM)
    shapes = [
        (rows, qw),
        (window_rows, qw),
        (window_rows, qw),
        (rows, cw),
        (token_rows, cw),
        (token_rows, cw),
    ]
    projected = pl.pallas_call(
        functools.partial(project_kernel, devices),
        out_shape=[pltpu.VMEM(shape, bf16) for shape in shapes],
        in_specs=[hbm, hbm, vmem, vmem, hbm, hbm, hbm],
        out_specs=[vmem] * 6,
        scratch_shapes=[
            pltpu.VMEM((window_rows, width), bf16),
            pltpu.VMEM((token_rows, context.shape[1]), bf16),
            pltpu.VMEM((2, 1, blocks), jnp.int32),
            pltpu.VMEM((window_rows, width), bf16),
            pltpu.VMEM(qkv_weight.shape, bf16),
            pltpu.VMEM(cross_query_weight.shape, bf16),
            pltpu.VMEM(cross_kv_weight.shape, bf16),
            pltpu.SemaphoreType.DMA((2,)),
            pltpu.SemaphoreType.DMA((5,)),
            pltpu.SemaphoreType.DMA((2, 3)),
            pltpu.SemaphoreType.DMA((2, 3)),
        ],
        compiler_params=pltpu.CompilerParams(
            collective_id=0, has_side_effects=True, vmem_limit_bytes=PROJECT_VMEM
        ),
        name="project",
    )(
        frames,
        context,
        noise_level.reshape(1, blocks),
        mod_table,
        qkv_weight,
        cross_query_weight,
        cross_kv_weight,
    )
    me = lax.axis_index("seq").astype(jnp.int32).reshape(1)
    return pl.pallas_call(
        functools.partial(attend_kernel, devices),
        out_shape=jax.ShapeDtypeStruct((rows, width), bf16),
        in_specs=[smem] * 6 + [vmem] * 8,
        out_specs=vmem,
        scratch_shapes=[
            pltpu.VMEM((window_rows, PAIR), bf16),
            pltpu.VMEM((rows, qw), bf16),
            pltpu.VMEM((rows, cw), bf16),
        ],
        compiler_params=pltpu.CompilerParams(vmem_limit_bytes=VMEM_LIMIT),
        name="attend",
    )(
        me,
        band_width,
        banded_attender_factor,
        cross_temp,
        alignment.T,
        counts,
        *projected,
        out_weight,
        cross_out_weight,
    )


def solution(mesh):
    placed = (
        P(("groups", "seq"), None),
        P(("groups", "seq"), None),
        P(("groups", "seq")),
        P(("groups", "seq"), None),
        P(("groups", "seq")),
        P(),
        P(),
        P(),
        P(),
        P(),
        P(),
        P(),
        P(),
        P(),
    )
    return jax.shard_map(
        shards, mesh=mesh, in_specs=placed, out_specs=P(("groups", "seq"), None), check_vma=False
    )
```

```python
import functools
import math

import jax
import jax.numpy as jnp
from jax import lax
from jax.experimental import pallas as pl
from jax.experimental.pallas import tpu as pltpu
from jax.sharding import PartitionSpec as P

BANDED_ATTEND_CT = 16
MIXED_ATTEND_CNT = 8
HD = 64
LEVELS = 8
BLK = 128
WMAX = 2
TOKB = 48
RCH = 1
ALIST = 2
PAIR = 2 * HD
HALO = WMAX * BLK
CHUNK = 256
SLAB = 32
EPS = 1e-06
VMEM_LIMIT = 32 * 1024 * 1024
PROJECT_VMEM = 54 * 1024 * 1024
SAFE_FACTOR = 6.0
MESH = pl.DeviceIdType.MESH


def pair_norm(part):
    low = lax.broadcasted_iota(jnp.int32, part.shape, 1) < HD
    square = part * part
    first = jnp.sum(jnp.where(low, square, 0.0), axis=-1, keepdims=True)
    second = jnp.sum(jnp.where(low, 0.0, square), axis=-1, keepdims=True)
    mean = jnp.where(low, first, second) * (1.0 / HD)
    return part * lax.rsqrt(mean + EPS)


def project_kernel(
    devices,
    frames,
    context,
    noise,
    mod,
    wqkv,
    wcq,
    wckv,
    q_out,
    k_out,
    v_out,
    cq_out,
    ck_out,
    cv_out,
    window,
    tokens,
    noise_halo,
    hidden,
    wqkv_v,
    wcq_v,
    wckv_v,
    local_sem,
    weight_sem,
    send_sem,
    recv_sem,
):
    me = lax.axis_index("seq")
    rows, width = frames.shape
    blocks = rows // BLK
    token_rows = context.shape[0]
    margin = RCH * TOKB
    qw = q_out.shape[1]
    cw = cq_out.shape[1]
    has = (me > 0, me < devices - 1)

    fetch_frames = pltpu.make_async_copy(
        frames, window.at[pl.ds(HALO, rows), :], local_sem.at[0]
    )
    fetch_tokens = pltpu.make_async_copy(
        context, tokens.at[pl.ds(margin, token_rows), :], local_sem.at[1]
    )
    fetch_frames.start()
    weight_order = (1, 2, 0)
    fetch_w = {}
    for slot in weight_order:
        cols = pl.ds(slot * qw, qw)
        fetch_w[slot] = pltpu.make_async_copy(
            wqkv.at[:, cols], wqkv_v.at[:, cols], weight_sem.at[slot]
        )
        fetch_w[slot].start()
    fetch_cq = pltpu.make_async_copy(wcq, wcq_v, weight_sem.at[3])
    fetch_ckv = pltpu.make_async_copy(wckv, wckv_v, weight_sem.at[4])

    barrier = pltpu.get_barrier_semaphore()
    for side in (0, 1):

        @pl.when(has[side])
        def _(side=side):
            pl.semaphore_signal(
                barrier, inc=1, device_id={"seq": me + 2 * side - 1}, device_id_type=MESH
            )

    peers = jnp.minimum(me, 1) + jnp.minimum(devices - 1 - me, 1)
    pl.semaphore_wait(barrier, peers)

    def copies(side):
        other = 1 - side
        peer = {"seq": me + 2 * side - 1}
        edge = rows - HALO if side else 0
        land = 0 if side else HALO + rows
        token_edge = token_rows - margin if side else 0
        token_land = 0 if side else margin + token_rows
        triples = (
            (noise, noise_halo.at[other]),
            (
                context.at[pl.ds(token_edge, margin), :],
                tokens.at[pl.ds(token_land, margin), :],
            ),
            (frames.at[pl.ds(edge, HALO), :], window.at[pl.ds(land, HALO), :]),
        )
        return [
            pltpu.make_async_remote_copy(
                src_ref=source,
                dst_ref=target,
                send_sem=send_sem.at[side, index],
                recv_sem=recv_sem.at[other, index],
                device_id=peer,
                device_id_type=MESH,
            )
            for index, (source, target) in enumerate(triples)
        ]

    sends = [copies(0), copies(1)]
    for side in (0, 1):

        @pl.when(has[side])
        def _(side=side):
            for copy in sends[side]:
                copy.start()

    fetch_cq.start()
    fetch_ckv.start()
    fetch_tokens.start()

    def make_hidden(row, level):
        scale = jnp.zeros((1, width), jnp.float32)
        shift = jnp.zeros((1, width), jnp.float32)
        for entry in range(LEVELS):
            here = level == entry
            scale = jnp.where(here, mod[entry : entry + 1, :width], scale)
            shift = jnp.where(here, mod[entry : entry + 1, width:], shift)
        for slab in range(BLK // SLAB):
            place = pl.ds(pl.multiple_of(row + slab * SLAB, SLAB), SLAB)
            values = window[place, :].astype(jnp.float32)
            mean = jnp.mean(values * values, axis=1, keepdims=True)
            normed = values * lax.rsqrt(mean + EPS)
            hidden[place, :] = (normed * (1.0 + scale) + shift).astype(jnp.bfloat16)

    def project(source, place, jobs):
        total = jobs[0][3].shape[1]

        def step(index, carry):
            out_cols = pl.multiple_of(index * CHUNK, CHUNK)
            for target_place, weight, first_col, target, normalize in jobs:
                y = jnp.dot(
                    source[place, :],
                    weight[:, pl.ds(pl.multiple_of(first_col + index * CHUNK, CHUNK), CHUNK)],
                    preferred_element_type=jnp.float32,
                )
                for part in range(CHUNK // PAIR):
                    piece = y[:, part * PAIR : (part + 1) * PAIR]
                    if normalize:
                        piece = pair_norm(piece)
                    target[target_place, pl.ds(out_cols + part * PAIR, PAIR)] = piece.astype(
                        jnp.bfloat16
                    )
            return carry

        lax.fori_loop(0, total // CHUNK, step, 0)

    fetch_frames.wait()
    for block in range(blocks):
        make_hidden(HALO + block * BLK, noise[:, block : block + 1])
    local = pl.ds(HALO, rows)
    for slot in weight_order:
        fetch_w[slot].wait()
    inner = pl.ds(0, rows)
    project(
        hidden,
        local,
        (
            (local, wqkv_v, qw, k_out, True),
            (local, wqkv_v, 2 * qw, v_out, False),
            (inner, wqkv_v, 0, q_out, True),
        ),
    )
    fetch_cq.wait()
    project(hidden, local, ((inner, wcq_v, 0, cq_out, True),))

    fetch_ckv.wait()
    fetch_tokens.wait()
    for side in (0, 1):
        token_place = pl.ds(side * (margin + token_rows), margin)

        @pl.when(has[side])
        def _(side=side, token_place=token_place):
            ref = tokens.at[token_place, :]
            pltpu.make_async_copy(ref, ref, recv_sem.at[side, 1]).wait()

        @pl.when(jnp.logical_not(has[side]))
        def _(token_place=token_place):
            tokens[token_place, :] = jnp.zeros((margin, tokens.shape[1]), jnp.bfloat16)

    every = pl.ds(0, tokens.shape[0])
    project(
        tokens,
        every,
        ((every, wckv_v, 0, ck_out, True), (every, wckv_v, cw, cv_out, False)),
    )

    def halo_step(step, carry):
        side = lax.rem(me + 1 + step, 2)
        present = jnp.where(side == 0, me > 0, me < devices - 1)
        row = pl.multiple_of(side * (HALO + rows), BLK)

        @pl.when(present)
        def _():
            for index, ref in ((0, noise_halo.at[0]), (2, window.at[pl.ds(0, HALO), :])):
                pltpu.make_async_copy(ref, ref, recv_sem.at[side, index]).wait()
            levels = noise_halo[side]
            for block in range(WMAX):
                low_side = levels[:, blocks - WMAX + block : blocks - WMAX + block + 1]
                level = jnp.where(side == 0, low_side, levels[:, block : block + 1])
                make_hidden(row + block * BLK, level)

        @pl.when(jnp.logical_not(present))
        def _():
            hidden[pl.ds(row, HALO), :] = jnp.zeros((HALO, width), jnp.bfloat16)

        place = pl.ds(row, HALO)
        project(
            hidden,
            place,
            ((place, wqkv_v, qw, k_out, True), (place, wqkv_v, 2 * qw, v_out, False)),
        )
        return carry

    lax.fori_loop(0, 2, halo_step, 0)

    for side in (0, 1):

        @pl.when(has[side])
        def _(side=side):
            for copy in sends[side]:
                copy.wait_send()


def attend_kernel(
    devices,
    me_ref,
    band,
    factor,
    temp,
    alignment,
    counts,
    q,
    k,
    v,
    cq,
    ck,
    cv,
    wo,
    wco,
    out,
    ones,
    self_out,
    cross_out,
):
    me = me_ref[0]
    rows = q.shape[0]
    blocks = rows // BLK
    window_rows = k.shape[0]
    span = ALIST * TOKB
    to_base2 = HD ** (-0.5) * math.log2(math.e)

    def half(shape, parity):
        lane = lax.broadcasted_iota(jnp.int32, shape, 1)
        return (lane < HD) if parity == 0 else (lane >= HD)

    def scores_of(query, key):
        return lax.dot_general(
            query, key, (((1,), (1,)), ((), ())), preferred_element_type=jnp.float32
        )

    def shifted_powers(scores, allowed):
        scores = jnp.where(allowed, scores, -jnp.inf)
        return jnp.exp2(scores - jnp.max(scores, axis=-1, keepdims=True))

    row_block = (
        lax.broadcasted_iota(jnp.int32, (window_rows, PAIR), 0) // BLK + me * blocks - WMAX
    )
    valid = (row_block >= 0) & (row_block < devices * blocks)
    ones[...] = jnp.where(valid, 1.0, 0.0).astype(jnp.bfloat16)

    def half_query(source, block, cols, parity):
        query = source[pl.ds(block * BLK, BLK), cols]
        return jnp.where(half(query.shape, parity), query, jnp.zeros_like(query))

    def merge(first, second):
        low = half(first.shape, 0)
        total = pltpu.roll(jnp.where(low, second, first), HD, 1)
        return (jnp.where(low, first, second) / total).astype(jnp.bfloat16)

    def self_pair(pair, carry):
        cols = pl.ds(pl.multiple_of(pair * PAIR, PAIR), PAIR)
        reaches = [band[2 * pair + parity] for parity in (0, 1)]
        scales = [factor[2 * pair + parity] * to_base2 for parity in (0, 1)]
        safe = (factor[2 * pair] <= SAFE_FACTOR) & (factor[2 * pair + 1] <= SAFE_FACTOR)

        def tiles(query, block, first, last):
            keys = pl.ds((block + WMAX + first) * BLK, (last - first) * BLK)
            return scores_of(query, k[keys, cols])

        def fast(sizes):
            for block in range(blocks):
                queries = [half_query(q, block, cols, parity) for parity in (0, 1)]
                common = min(sizes)
                shared = tiles(jnp.concatenate(queries, axis=0), block, -common, common + 1)
                sums = []
                for parity in (0, 1):
                    size = sizes[parity]
                    keys = pl.ds((block + WMAX - size) * BLK, (2 * size + 1) * BLK)
                    scores = shared[parity * BLK : (parity + 1) * BLK, :]
                    if size > common:
                        left = tiles(queries[parity], block, -size, -common)
                        right = tiles(queries[parity], block, common + 1, size + 1)
                        scores = jnp.concatenate([left, scores, right], axis=1)
                    powers = jnp.exp2(scores * scales[parity])
                    value = v[keys, cols]
                    value = jnp.where(half(value.shape, parity), value, ones[keys, :])
                    sums.append(
                        jnp.dot(
                            powers.astype(jnp.bfloat16), value, preferred_element_type=jnp.float32
                        )
                    )
                self_out[pl.ds(block * BLK, BLK), cols] = merge(*sums)

        for low_size in range(WMAX + 1):
            for high_size in range(WMAX + 1):
                pl.when(safe & (reaches[0] == low_size) & (reaches[1] == high_size))(
                    functools.partial(fast, (low_size, high_size))
                )

        @pl.when(jnp.logical_not(safe))
        def _():
            def one(block, inner):
                first = pl.multiple_of(block * BLK, BLK)
                keys = pl.ds(first, (2 * WMAX + 1) * BLK)
                sums = []
                for parity in (0, 1):
                    query = q[pl.ds(first, BLK), cols]
                    query = jnp.where(half(query.shape, parity), query, jnp.zeros_like(query))
                    scores = scores_of(query, k[keys, cols]) * scales[parity]
                    offset = lax.broadcasted_iota(jnp.int32, scores.shape, 1) // BLK - WMAX
                    key_block = offset + block + me * blocks
                    allowed = (
                        (jnp.abs(offset) <= reaches[parity])
                        & (key_block >= 0)
                        & (key_block < devices * blocks)
                    )
                    value = v[keys, cols]
                    value = jnp.where(half(value.shape, parity), value, ones[keys, :])
                    sums.append(
                        jnp.dot(
                            shifted_powers(scores, allowed).astype(jnp.bfloat16),
                            value,
                            preferred_element_type=jnp.float32,
                        )
                    )
                self_out[pl.ds(first, BLK), cols] = merge(*sums)
                return inner

            lax.fori_loop(0, blocks, one, 0)

        return carry

    lax.fori_loop(0, BANDED_ATTEND_CT // 2, self_pair, 0)

    token_blocks = ck.shape[0] // TOKB - 2 * RCH

    def cross_pair(pair, carry):
        cols = pl.ds(pl.multiple_of(pair * PAIR, PAIR), PAIR)
        scales = [temp[2 * pair + parity] * to_base2 for parity in (0, 1)]
        safe = (temp[2 * pair] <= SAFE_FACTOR) & (temp[2 * pair + 1] <= SAFE_FACTOR)

        def run(shifted):
            for block in range(blocks):
                listed = [alignment[slot, block] for slot in range(ALIST)]
                lowest = jnp.minimum(listed[0], listed[1])
                live = counts[block]
                admit = [
                    jnp.where(
                        ((listed[0] == lowest + slot) & (live > 0))
                        | ((listed[1] == lowest + slot) & (live > 1)),
                        1,
                        0,
                    )
                    for slot in range(ALIST)
                ]
                start = (lowest - (me * token_blocks - RCH)) * TOKB
                place = pl.ds(pl.multiple_of(start, 16), span)
                row = lax.broadcasted_iota(jnp.int32, (span, PAIR), 0)
                row_ok = jnp.where(row < TOKB, admit[0], admit[1]) > 0
                queries = [half_query(cq, block, cols, parity) for parity in (0, 1)]
                both = scores_of(jnp.concatenate(queries, axis=0), ck[place, cols])
                sums = []
                for parity in (0, 1):
                    scores = both[parity * BLK : (parity + 1) * BLK, :] * scales[parity]
                    value = cv[place, cols]
                    value = jnp.where(half(value.shape, parity), value, jnp.ones_like(value))
                    value = jnp.where(row_ok, value, jnp.zeros_like(value))
                    if shifted:
                        token = lax.broadcasted_iota(jnp.int32, scores.shape, 1)
                        ok = jnp.where(token < TOKB, admit[0], admit[1]) > 0
                        powers = shifted_powers(scores, ok)
                    else:
                        powers = jnp.exp2(scores)
                    sums.append(
                        jnp.dot(
                            powers.astype(jnp.bfloat16), value, preferred_element_type=jnp.float32
                        )
                    )
                cross_out[pl.ds(block * BLK, BLK), cols] = merge(*sums)

        pl.when(safe)(functools.partial(run, False))
        pl.when(jnp.logical_not(safe))(functools.partial(run, True))
        return carry

    lax.fori_loop(0, MIXED_ATTEND_CNT // 2, cross_pair, 0)
    def finish(index, carry):
        cols = pl.ds(pl.multiple_of(index * CHUNK, CHUNK), CHUNK)
        total = jnp.dot(self_out[...], wo[:, cols], preferred_element_type=jnp.float32)
        total += jnp.dot(cross_out[...], wco[:, cols], preferred_element_type=jnp.float32)
        out[:, cols] = total.astype(jnp.bfloat16)
        return carry

    lax.fori_loop(0, out.shape[1] // CHUNK, finish, 0)


def shards(
    frames,
    context,
    noise_level,
    alignment,
    counts,
    band_width,
    mod_table,
    qkv_weight,
    out_weight,
    cross_query_weight,
    cross_kv_weight,
    cross_out_weight,
    banded_attender_factor,
    cross_temp,
):
    rows, width = frames.shape
    blocks = rows // BLK
    qw = qkv_weight.shape[1] // 3
    cw = cross_query_weight.shape[1]
    devices = lax.axis_size("seq")
    window_rows = rows + 2 * HALO
    token_rows = context.shape[0] + 2 * RCH * TOKB
    bf16 = jnp.bfloat16
    hbm = pl.BlockSpec(memory_space=pltpu.HBM)
    vmem = pl.BlockSpec(memory_space=pltpu.VMEM)
    smem = pl.BlockSpec(memory_space=pltpu.SMEM)
    shapes = [
        (rows, qw),
        (window_rows, qw),
        (window_rows, qw),
        (rows, cw),
        (token_rows, cw),
        (token_rows, cw),
    ]
    projected = pl.pallas_call(
        functools.partial(project_kernel, devices),
        out_shape=[pltpu.VMEM(shape, bf16) for shape in shapes],
        in_specs=[hbm, hbm, vmem, vmem, hbm, hbm, hbm],
        out_specs=[vmem] * 6,
        scratch_shapes=[
            pltpu.VMEM((window_rows, width), bf16),
            pltpu.VMEM((token_rows, context.shape[1]), bf16),
            pltpu.VMEM((2, 1, blocks), jnp.int32),
            pltpu.VMEM((window_rows, width), bf16),
            pltpu.VMEM(qkv_weight.shape, bf16),
            pltpu.VMEM(cross_query_weight.shape, bf16),
            pltpu.VMEM(cross_kv_weight.shape, bf16),
            pltpu.SemaphoreType.DMA((2,)),
            pltpu.SemaphoreType.DMA((5,)),
            pltpu.SemaphoreType.DMA((2, 3)),
            pltpu.SemaphoreType.DMA((2, 3)),
        ],
        compiler_params=pltpu.CompilerParams(
            collective_id=0, has_side_effects=True, vmem_limit_bytes=PROJECT_VMEM
        ),
        name="project",
    )(
        frames,
        context,
        noise_level.reshape(1, blocks),
        mod_table,
        qkv_weight,
        cross_query_weight,
        cross_kv_weight,
    )
    me = lax.axis_index("seq").astype(jnp.int32).reshape(1)
    return pl.pallas_call(
        functools.partial(attend_kernel, devices),
        out_shape=jax.ShapeDtypeStruct((rows, width), bf16),
        in_specs=[smem] * 6 + [vmem] * 8,
        out_specs=vmem,
        scratch_shapes=[
            pltpu.VMEM((window_rows, PAIR), bf16),
            pltpu.VMEM((rows, qw), bf16),
            pltpu.VMEM((rows, cw), bf16),
        ],
        compiler_params=pltpu.CompilerParams(vmem_limit_bytes=VMEM_LIMIT),
        name="attend",
    )(
        me,
        band_width,
        banded_attender_factor,
        cross_temp,
        alignment.T,
        counts,
        *projected,
        out_weight,
        cross_out_weight,
    )


def solution(mesh):
    placed = (
        P(("groups", "seq"), None),
        P(("groups", "seq"), None),
        P(("groups", "seq")),
        P(("groups", "seq"), None),
        P(("groups", "seq")),
        P(),
        P(),
        P(),
        P(),
        P(),
        P(),
        P(),
        P(),
        P(),
    )
    return jax.shard_map(
        shards, mesh=mesh, in_specs=placed, out_specs=P(("groups", "seq"), None), check_vma=False
    )
```
